512 devices in a mesh: depth: 4 (over x), row: 8 (over z_hi, core), col: 16 (over z_lo, y).
Axes of the slice: x: 4, y: 8, z: 8 (z_hi: 4, z_lo: 2; z = z_hi * 2 + z_lo), core: 2. Of those that a mesh axis runs over, the one named last changes fastest.
Arguments:
- tokens: bfloat16 [512, 6144], P(('depth', 'row'), 'col'), may hold values from -6 to 6
- grad_out: bfloat16 [512, 6144], P(('depth', 'row'), 'col'), may hold values from -6 to 6
- w_up: bfloat16 [6144, 24576], P(('col', 'depth'), 'row'), may hold values from -0.078125 to 0.078125
- w_down: bfloat16 [6144, 24576], P(('col', 'depth'), 'row'), may hold values from -0.0390625 to 0.0390625
Outputs:
- grad_in: bfloat16 [512, 6144], P(('depth', 'row'), 'col')
- grad_up: bfloat16 [6144, 24576], P(('col', 'depth'), 'row')
- grad_down: bfloat16 [6144, 24576], P(('col', 'depth'), 'row')
The draws below stay inside these ranges and needn't reach their ends.
All inputs are finite; a program needn't handle non-finite values.
Results may differ from the reference program's by a relative error of at most 0.03.
Values may be sent and summed in bfloat16 or wider, within the bound.
No kernel may reach another device: no remote copies, remote signals or barrier semaphores. Data moves between devices by JAX's collectives and lax.ppermute only.
A program may use at most 64 MiB of HBM per device.

```python
import math
import jax
import jax.numpy as jnp
from jax import lax

D = 6144
FF = 24576
TOK_DEV = 128
TOKENS = 512
D_PART = 384
N_DEPTH = 4
N_COL = 16


def raised(entries, rng, source, target, blocks, factor):
    def block_of(axis_at):
        return (jnp.arange(entries.shape[axis_at]) // (entries.shape[axis_at] // blocks)).reshape((-1,) + (1,) * (entries.ndim - 1 - axis_at))

    one_side = jax.random.permutation(rng, blocks)[block_of(target)]
    far = (block_of(target) + blocks // 2) % blocks
    return jnp.where((block_of(source) == one_side) | (block_of(source) == far), factor * entries, entries)


def levels(stream_key, dims, cuts, least, top_value):
    gain, own = 1.0, jax.random.fold_in(stream_key, 6)
    for dim, shards_of in cuts:
        draws = jnp.exp(jax.random.uniform(jax.random.fold_in(own, dim), (shards_of,), jnp.float32, least / len(cuts), top_value / len(cuts)))
        gain = gain * jnp.repeat(draws, dims[dim] // shards_of).reshape([-1 if axis == dim else 1 for axis in range(len(dims))])
    return gain


def bell_draw(key, dims, width, most, shards=(), kind=jnp.bfloat16):
    values = jax.random.normal(key, dims, jnp.float32) * width
    if len(shards) > 0:
        values = levels(key, dims, shards, -0.22, 0.18) * values
    return jnp.clip(values, min=-most, max=most).astype(kind)


def bell_draw_with(key, dims, spread, bound, split, heavy, held_as=jnp.bfloat16):
    entries = spread * jax.random.normal(key, dims, jnp.float32)
    if split:
        entries = entries * levels(key, dims, split, -0.22, 0.18)
    return jnp.clip(raised(entries, jax.random.fold_in(key, 3), *heavy), -bound, bound).astype(held_as)


def setup_inputs(seed: int = 0) -> dict:
    streams_of = jax.random.split(jax.random.key(seed), 5)
    return {
        "tokens": bell_draw_with(streams_of[0], (TOKENS, D), 1.0, 6.0, ((0, 32), (1, 16)), (0, 1, 32, 2.75)),
        "grad_out": bell_draw(streams_of[1], (TOKENS, D), 1.0, 6.0, ((0, 32), (1, 16))),
        "w_up": bell_draw(streams_of[2], (D, FF), D ** -0.5, 0.078125, ((0, 64), (1, 8))),
        "w_down": bell_draw(streams_of[3], (D, FF), FF ** -0.5, 0.0390625, ((0, 64), (1, 8))),
    }


def gelu_parts(hidden):
    coeff = math.sqrt(2.0 / math.pi)
    cube = hidden * hidden * hidden
    slope_in = jnp.tanh(coeff * (hidden + 0.044715 * cube))
    value = 0.5 * hidden * (1.0 + slope_in)
    slope = 0.5 * (1.0 + slope_in) + 0.5 * hidden * (1.0 - slope_in * slope_in) * coeff * (1.0 + 3.0 * 0.044715 * hidden * hidden)
    return (value, slope)

def block_sum(left, weight):
    left_blocks = jnp.transpose(left.reshape(TOKENS, N_COL, D_PART), (1, 0, 2))
    weight_blocks = weight.reshape(N_COL, D_PART, FF)

    def add_block(carry, pieces):
        part = jnp.dot(pieces[0], pieces[1], preferred_element_type=jnp.float32)
        part = lax.optimization_barrier(part.astype(jnp.bfloat16)).astype(jnp.float32)
        return (carry + part, None)
    total, unused = lax.scan(add_block, jnp.zeros((TOKENS, FF), jnp.float32), (left_blocks, weight_blocks))
    return total

def reference(tokens, grad_out, w_up, w_down):
    hidden_pre = block_sum(tokens, w_up)
    act_value, slope = gelu_parts(hidden_pre)
    act = act_value.astype(jnp.bfloat16)
    act_grad = block_sum(grad_out, w_down)
    hidden_grad = (act_grad * slope).astype(jnp.bfloat16)
    grad_in = jnp.dot(hidden_grad, w_up.T, preferred_element_type=jnp.float32).astype(jnp.bfloat16)
    token_blocks = tokens.reshape(N_DEPTH, TOK_DEV, D)
    grad_blocks = hidden_grad.reshape(N_DEPTH, TOK_DEV, FF)

    def add_quarter(carry, pieces):
        part = jnp.dot(pieces[0].T, pieces[1], preferred_element_type=jnp.float32)
        part = lax.optimization_barrier(part.astype(jnp.bfloat16)).astype(jnp.float32)
        return (carry + part, None)
    grad_up_sum, unused = lax.scan(add_quarter, jnp.zeros((D, FF), jnp.float32), (token_blocks, grad_blocks))
    grad_up = grad_up_sum.astype(jnp.bfloat16)
    grad_down = jnp.dot(grad_out.T, act, preferred_element_type=jnp.float32).astype(jnp.bfloat16)
    return (grad_in, grad_up, grad_down)
```

```python
import math

import jax
import jax.numpy as jnp
from jax import lax
from jax.sharding import Mesh, PartitionSpec as P

bf16, f32 = jnp.bfloat16, jnp.float32
ROW = ("zhi", "core")
COL = ("zlo", "y")


def gelu_parts(hidden):
    coeff = math.sqrt(2.0 / math.pi)
    cube = hidden * hidden * hidden
    slope_in = jnp.tanh(coeff * (hidden + 0.044715 * cube))
    value = 0.5 * hidden * (1.0 + slope_in)
    slope = 0.5 * (1.0 + slope_in) + 0.5 * hidden * (1.0 - slope_in * slope_in) * coeff * (
        1.0 + 3.0 * 0.044715 * hidden * hidden
    )
    return (value, slope)


def after(value, *others):
    return lax.optimization_barrier((value,) + others)[0]


def contract(left, right, left_at, right_at):
    return lax.dot_general(
        left, right, (((left_at,), (right_at,)), ((), ())), preferred_element_type=f32
    )


def body(tokens, grad_out, w_up, w_down):
    n_depth = lax.axis_size("depth")
    n_row = lax.axis_size("zhi") * lax.axis_size("core")
    n_y = lax.axis_size("y")
    depth_pos = lax.axis_index("depth")
    pair_pos = lax.axis_index("zlo")
    narrow, hidden = w_up.shape
    own_rows, feats = tokens.shape
    group = own_rows * n_row
    half = group // 2
    piece = half // n_y

    def from_ahead(array, j):
        return lax.ppermute(array, "depth", [(i, (i - j) % n_depth) for i in range(n_depth)])

    def to_ahead(array, j):
        return lax.ppermute(array, "depth", [(i, (i + j) % n_depth) for i in range(n_depth)])

    def swap(array):
        return lax.ppermute(array, "zlo", [(0, 1), (1, 0)])

    def exchange(array, axis):
        return lax.all_to_all(array, axis, 0, 0, tiled=True)

    def copies(array, count):
        return jnp.broadcast_to(array[None], (count,) + array.shape)

    def rolled(array, start, axis):
        return lax.dynamic_slice_in_dim(
            jnp.concatenate([array, array], axis), start, array.shape[axis], axis
        )

    def gather(array):
        return jnp.concatenate([array] + [from_ahead(array, j) for j in range(1, n_depth)], 0)

    def summed(got):
        return jnp.sum(got.astype(f32), axis=0)

    up_block = exchange(copies(w_up, n_depth), "depth").reshape(feats, hidden)
    both = lax.all_gather(jnp.stack([tokens, grad_out]), ROW, axis=0)
    x_rows = both[:, 0].reshape(group, feats)
    dy_rows = rolled(both[:, 1].reshape(group, feats), pair_pos * half, 0)
    x_rot = rolled(x_rows, depth_pos * narrow, 1)
    dy_rot = rolled(dy_rows, depth_pos * narrow, 1)
    down_block = lax.all_gather(after(w_down, both), "depth", axis=0, tiled=True)

    pre_part = contract(x_rows, up_block, 1, 0).astype(bf16)
    sent = pre_part.reshape(2 * n_y, piece, hidden)
    pre = summed(exchange(sent, COL))
    act_value, slope = gelu_parts(pre)
    act_near = exchange(copies(act_value.astype(bf16), n_y), "y").reshape(half, hidden)

    grad_part = contract(dy_rows, after(down_block, pre_part), 1, 0).astype(bf16)
    grad_other = swap(grad_part[half:])
    grad_pair = (grad_part[:half].astype(f32) + grad_other.astype(f32)).astype(bf16)
    grad_pair = after(grad_pair, act_near).reshape(n_y, piece, hidden)
    act = jnp.concatenate([act_near, swap(act_near)], 0)
    down_part = contract(dy_rows, act, 0, 0).astype(bf16)
    act_grad = summed(exchange(grad_pair, "y"))
    mine = (act_grad * slope).astype(bf16)
    hidden_grad = exchange(copies(mine, 2 * n_y), COL).reshape(group, hidden)

    def scatter(part):
        return [part[:narrow]] + [
            to_ahead(part[j * narrow : (j + 1) * narrow], j) for j in range(1, n_depth)
        ]

    def total(parts):
        acc = parts[0].astype(f32)
        for part in parts[1:]:
            acc = acc + part.astype(f32)
        return acc.astype(bf16)

    grad_down = lax.psum_scatter(down_part, "depth", scatter_dimension=0, tiled=True)
    up_terms = scatter(contract(x_rot, hidden_grad, 0, 0).astype(bf16))
    grad_in_part = contract(hidden_grad, up_block, 1, 1).astype(bf16)
    grad_in_part = after(grad_in_part, up_terms[1])
    got = exchange(grad_in_part.reshape(n_row, own_rows, feats), ROW)
    grad_in = summed(got).astype(bf16)
    grad_up = total(up_terms)
    return (grad_in, grad_up, grad_down)


def solution(mesh):
    shape = mesh.devices.shape
    fine = Mesh(
        mesh.devices.reshape(shape[0], shape[1] // 2, 2, 2, shape[2] // 2),
        ("depth", "zhi", "core", "zlo", "y"),
    )
    tokens_at = P(("depth",) + ROW, ("zlo", "y"))
    weights_at = P(("zlo", "y", "depth"), ROW)
    return jax.shard_map(
        body,
        mesh=fine,
        in_specs=(tokens_at, tokens_at, weights_at, weights_at),
        out_specs=(tokens_at, weights_at, weights_at),
        check_vma=False,
    )
```

```python
import math

import jax
import jax.numpy as jnp
from jax import lax
from jax.experimental import pallas as pl
from jax.sharding import Mesh, PartitionSpec as P

bf16, f32 = jnp.bfloat16, jnp.float32
ROW = ("zhi", "core")
COL = ("zlo", "y")


def gelu_parts(hidden):
    coeff = math.sqrt(2.0 / math.pi)
    cube = hidden * hidden * hidden
    slope_in = jnp.tanh(coeff * (hidden + 0.044715 * cube))
    value = 0.5 * hidden * (1.0 + slope_in)
    slope = 0.5 * (1.0 + slope_in) + 0.5 * hidden * (1.0 - slope_in * slope_in) * coeff * (
        1.0 + 3.0 * 0.044715 * hidden * hidden
    )
    return (value, slope)


def tie(*values):
    return lax.optimization_barrier(values)


def contract(left, right, left_at, right_at):
    return lax.dot_general(
        left, right, (((left_at,), (right_at,)), ((), ())), preferred_element_type=f32
    )


TILE = 1024


def tiled_call(kernel, left, rights, out_rows, flops):
    cols = rights[0].shape[1]
    moved = 2 * cols * (sum(r.shape[0] for r in rights) + sum(out_rows))
    return pl.pallas_call(
        kernel,
        grid=(cols // TILE,),
        in_specs=[pl.BlockSpec(left.shape, lambda j: (0, 0))]
        + [pl.BlockSpec((r.shape[0], TILE), lambda j: (0, j)) for r in rights],
        out_specs=[pl.BlockSpec((n, TILE), lambda j: (0, j)) for n in out_rows],
        out_shape=[jax.ShapeDtypeStruct((n, cols), bf16) for n in out_rows],
        cost_estimate=pl.CostEstimate(flops=flops, transcendentals=0, bytes_accessed=moved),
    )(left, *rights)


def matmul_parts(left, rights, out_rows, transposed):
    count = len(rights)

    def kernel(left_ref, *refs):
        stacked = jnp.concatenate([ref[...] for ref in refs[:count]], 0)
        result = contract(left_ref[...], stacked, 0 if transposed else 1, 0).astype(bf16)
        start = 0
        for ref in refs[count:]:
            ref[...] = result[start : start + ref.shape[0]]
            start += ref.shape[0]

    flops = 2 * left.shape[0] * left.shape[1] * rights[0].shape[1]
    return tiled_call(kernel, left, rights, out_rows, flops)


def body(tokens, grad_out, w_up, w_down):
    n_depth = lax.axis_size("depth")
    n_row = lax.axis_size("zhi") * lax.axis_size("core")
    n_y = lax.axis_size("y")
    depth_pos = lax.axis_index("depth")
    pair_pos = lax.axis_index("zlo")
    narrow, hidden = w_up.shape
    own_rows, feats = tokens.shape
    group = own_rows * n_row
    half = group // 2
    piece = half // n_y

    def from_ahead(array, j):
        return lax.ppermute(array, "depth", [(i, (i - j) % n_depth) for i in range(n_depth)])

    def to_ahead(array, j):
        return lax.ppermute(array, "depth", [(i, (i + j) % n_depth) for i in range(n_depth)])

    def swap(array):
        return lax.ppermute(array, "zlo", [(0, 1), (1, 0)])

    def exchange(array, axis):
        return lax.all_to_all(array, axis, 0, 0, tiled=True)

    def copies(array, count):
        return jnp.broadcast_to(array[None], (count,) + array.shape)

    def rolled(array, start, axis):
        return lax.dynamic_slice_in_dim(
            jnp.concatenate([array, array], axis), start, array.shape[axis], axis
        )

    def gather(array):
        return jnp.concatenate([array] + [from_ahead(array, j) for j in range(1, n_depth)], 0)

    def summed(got):
        return jnp.sum(got.astype(f32), axis=0)

    up_block = exchange(copies(w_up, n_depth), "depth").reshape(feats, hidden)
    both = lax.all_gather(jnp.stack([tokens, grad_out]), ROW, axis=0)
    w_down, both = tie(w_down, both)
    x_rows = both[:, 0].reshape(group, feats)
    dy_rows = both[:, 1].reshape(group, feats)
    x_rot = rolled(x_rows, depth_pos * narrow, 1)
    dy_rot = rolled(dy_rows, depth_pos * narrow, 1)
    dy_swapped = rolled(dy_rot, pair_pos * half, 0)

    down_near, down_back = from_ahead(w_down, 1), from_ahead(w_down, n_depth - 1)
    pre_part = contract(x_rows, up_block, 1, 0).astype(bf16)
    got = exchange(pre_part.reshape(2 * n_y, piece, hidden), COL)
    got, down_near, down_back = tie(got, down_near, down_back)
    pre = summed(got)
    cut = narrow // 2
    far_top = from_ahead(down_near[:cut], 1)
    far_end = from_ahead(down_back[cut:], n_depth - 1)
    down_blocks = [w_down, down_near, far_top, far_end, down_back]
    act_value, slope = gelu_parts(pre)
    act_near = exchange(copies(act_value.astype(bf16), n_y), "y").reshape(half, hidden)
    held = tie(act_near, *down_blocks)
    act_near, down_blocks = held[0], held[1:]
    (grad_part,) = matmul_parts(dy_rot, down_blocks, [group], False)
    grad_part, act_far = tie(grad_part, swap(act_near))
    act_grad = summed(exchange(grad_part.reshape(2 * n_y, piece, hidden), COL))
    down_parts = matmul_parts(dy_swapped, [act_near, act_far], [narrow] * n_depth, True)
    mine = (act_grad * slope).astype(bf16)
    held = tie(mine, *down_parts)
    mine, down_parts = held[0], held[1:]
    hidden_grad = exchange(copies(mine, 2 * n_y), COL).reshape(group, hidden)

    def scatter(parts):
        return [parts[0]] + [to_ahead(parts[j], j) for j in range(1, n_depth)]

    def total(parts):
        acc = parts[0].astype(f32)
        for part in parts[1:]:
            acc = acc + part.astype(f32)
        return acc.astype(bf16)

    down_terms = scatter(down_parts)
    up_parts = matmul_parts(x_rot, [hidden_grad], [narrow] * n_depth, True)
    held = lax.optimization_barrier(tuple(up_parts) + tuple(down_terms))
    up_parts, down_terms = held[:n_depth], held[n_depth:]
    grad_down = total(down_terms)
    up_terms = scatter(up_parts)
    grad_in_part = contract(hidden_grad, up_block, 1, 1).astype(bf16)
    grad_in_part, up_terms[1] = tie(grad_in_part, up_terms[1])
    got = exchange(grad_in_part.reshape(n_row, own_rows, feats), ROW)
    grad_in = summed(got).astype(bf16)
    grad_up = total(up_terms)
    return (grad_in, grad_up, grad_down)


def solution(mesh):
    shape = mesh.devices.shape
    fine = Mesh(
        mesh.devices.reshape(shape[0], shape[1] // 2, 2, 2, shape[2] // 2),
        ("depth", "zhi", "core", "zlo", "y"),
    )
    tokens_at = P(("depth",) + ROW, ("zlo", "y"))
    weights_at = P(("zlo", "y", "depth"), ROW)
    return jax.shard_map(
        body,
        mesh=fine,
        in_specs=(tokens_at, tokens_at, weights_at, weights_at),
        out_specs=(tokens_at, weights_at, weights_at),
        check_vma=False,
    )
```
